32 devices in a mesh: grp: 2 (over y), pool: 8 (over z, core), tp: 2 (over x).
Axes of the slice: x: 2, y: 2, z: 4, core: 2. Of those that a mesh axis runs over, the one named last changes fastest.
Arguments:
- home_query: bfloat16 [64, 8192], P(('grp', 'pool'), 'tp'), parts along dimension 0, may hold values from -12 to 12
- home_key: bfloat16 [64, 1024], P(('grp', 'pool'), 'tp'), parts along dimension 0, may hold values from -5 to 5
- home_value: bfloat16 [64, 1024], P(('grp', 'pool'), 'tp'), parts along dimension 0, may hold values from -5 to 5
- cache_keys: bfloat16 [8192, 1024], P(('grp', 'pool'), 'tp'), parts along dimension 0, may hold values from -12 to 12
- cache_values: bfloat16 [8192, 1024], P(('grp', 'pool'), 'tp'), parts along dimension 0, may hold values from -5 to 5
- cache_start: int32 [64], P('grp'), parts along dimension 0, may hold values from 0 to 4088, as said below
- cache_len: int32 [64], P('grp'), parts along dimension 0, may hold values from 8 to 64, as said below
- prompt_query: bfloat16 [7168, 8192], P(('grp', 'pool'), 'tp'), parts along dimension 0, may hold values from -12 to 12
- prompt_key: bfloat16 [7168, 1024], P(('grp', 'pool'), 'tp'), parts along dimension 0, may hold values from -12 to 12
- prompt_value: bfloat16 [7168, 1024], P(('grp', 'pool'), 'tp'), parts along dimension 0, may hold values from -5 to 5
- doc_ids: int32 [16, 448], P(('grp', 'pool')), parts along dimension 0, may hold values from 0 to 3, never falling along the last dimension, each value on 1 to 224 neighbouring positions
- out_weight: bfloat16 [8192, 8192], P('tp', 'pool'), may hold values from -0.0625 to 0.0625
Outputs:
- prompt_out: bfloat16 [7168, 8192], P(('grp', 'pool'), 'tp'), parts along dimension 0
- decode_out: bfloat16 [64, 8192], P(('grp', 'tp'), 'pool'), parts along dimension 0
The draws below stay inside these ranges and needn't reach their ends.
There are 2 independent parts, one for each index of `grp`. The reference program is written for one: setup_inputs(seed, part) draws one part's arguments, and reference() takes and returns one part's arrays. A program takes and returns all parts, laid end to end along the dimension named above; an argument that names none is the same for every part. Nothing has to cross between parts.
Inputs may be any that keep to these rules, and one draw needn't show every extreme that they name: Each request's cache occupies cache_len rows from cache_start on, inside the 512 rows of one pool index and apart from every other request's rows; a pool index holds the caches of at most 8 requests, and some pool index of exactly 8. `cache_len`: some request has exactly 64 rows.
All inputs are finite; a program needn't handle non-finite values.
Results may differ from the reference program's by a relative error of at most 0.008.
Values may be sent and summed in bfloat16 or wider, within the bound.
A program may use at most 128 MiB of HBM per device.

```python
import math
import jax
import jax.numpy as jnp
import numpy as np
from jax import lax

D = 8192
HEADS = 64
KV_HEADS = 8
HEAD_DIM = 128
PRE_DEV = 448
CAP = 512
DOCS = 4
REQS = 32
MOST = 8
CACHE_MAX = 64
LMIN = 8
N_POOL = 8


def route_tables(key):
    slot_count = N_POOL * MOST
    full_owner = jax.random.randint(jax.random.fold_in(key, 11), (), 0, N_POOL)
    ranking_seed = jax.random.permutation(jax.random.fold_in(key, 12), slot_count)
    slot_owner = jnp.arange(slot_count) // MOST
    priority = ranking_seed - slot_count * (slot_owner == full_owner).astype(jnp.int32)
    ranking = jnp.argsort(priority, stable=True)
    chosen = ranking[:REQS]
    shuffle = jax.random.permutation(jax.random.fold_in(key, 13), REQS)
    slot_taken = chosen[shuffle]
    owner_of = slot_taken // MOST
    within = slot_taken % MOST
    lengths = jax.random.randint(jax.random.fold_in(key, 14), (REQS,), LMIN, CACHE_MAX + 1)
    lengths = jnp.where(slot_taken == ranking[0], CACHE_MAX, lengths)
    offsets = jax.random.randint(jax.random.fold_in(key, 15), (REQS,), 0, CACHE_MAX - lengths + 1)
    starts = owner_of * CAP + within * CACHE_MAX + offsets
    return (starts.astype(jnp.int32), lengths.astype(jnp.int32))


def marked_keys(key, salt, row_total):
    sampled = jax.random.truncated_normal(jax.random.fold_in(key, salt), -5.0, 5.0, (row_total, KV_HEADS * HEAD_DIM), jnp.float32)
    return sampled.astype(jnp.bfloat16)


def drawn_queries(key, salt, row_total):
    sampled = jax.random.truncated_normal(jax.random.fold_in(key, salt), -5.0, 5.0, (row_total, D), jnp.float32)
    return sampled.astype(jnp.bfloat16)


def draw_cache_start(key, part):
    return route_tables(key)[0]


def draw_cache_len(key, part):
    return route_tables(key)[1]


def draw_cache_keys(key, part):
    return marked_keys(key, 31, N_POOL * CAP)


def draw_prompt_key(key, part):
    return marked_keys(key, 32, N_POOL * PRE_DEV)


def draw_home_query(key, part):
    return drawn_queries(key, 33, REQS)


def draw_prompt_query(key, part):
    return drawn_queries(key, 34, N_POOL * PRE_DEV)


def steps_of(stream_key, dims, split, smallest, high):
    factor_of, own = 1.0, jax.random.fold_in(stream_key, 6)
    for position, shards_of in split:
        draws = jnp.exp(jax.random.uniform(jax.random.fold_in(own, position), (shards_of,), jnp.float32, smallest / len(split), high / len(split)))
        factor_of = factor_of * jnp.repeat(draws, dims[position] // shards_of).reshape([-1 if axis == position else 1 for axis in range(len(dims))])
    return factor_of


def profile(count, total, reach, lean):
    loads = [(1 << 20) // math.isqrt(grade ** lean) + 1 for grade in range(2, count + 1)]
    rest, given = total - reach - (count - 1), [1] * (count - 1)
    while rest > 0:
        candidates = [i for i in range(count - 1) if given[i] < reach]
        pool, left = sum([loads[i] for i in candidates]), rest
        for i in candidates:
            addition = min(reach - given[i], max(1, left * loads[i] // pool), rest)
            given[i] = given[i] + addition
            rest = rest - addition
    return np.array([reach] + given)


def ragged_sizes(key, amount, total, most, skew):
    if amount == 2:
        one = jax.random.randint(key, (), max(1, total - most), min(most, total - 1) + 1)
        return jnp.stack([one, total - one])
    tallies = jnp.asarray(profile(amount, total, most, skew), jnp.int32)
    couples = (amount - 1) // 2
    giver, taker = tallies[1:1 + 2 * couples:2], tallies[2:2 + 2 * couples:2]
    slack = jnp.minimum(giver - 1, most - taker)
    moved = jax.random.randint(jax.random.fold_in(key, 1), (couples,), 0, 1 << 20) % (slack + 1)
    tallies = tallies.at[1:1 + 2 * couples:2].set(giver - moved).at[2:2 + 2 * couples:2].set(taker + moved)
    return tallies[jax.random.permutation(jax.random.fold_in(key, 2), amount)]


def centred(stream_key, dims, scale, limit, split=(), kind=jnp.bfloat16):
    loudness = steps_of(stream_key, dims, split, -0.22, 0.18) if split else 1.0
    values = jax.random.normal(stream_key, dims, jnp.float32) * scale * loudness
    return jnp.minimum(jnp.maximum(values, -limit), limit).astype(kind)


def setup_inputs(seed: int = 0, part: int = 0) -> dict:
    splits = jax.random.split(jax.random.key(seed), 13)
    part_splits = jax.random.split(jax.random.fold_in(splits[12], part), 13)
    return {
        "home_query": draw_home_query(jax.random.fold_in(jax.random.fold_in(splits[12], part), 71), part),
        "home_key": centred(part_splits[1], (REQS, KV_HEADS * HEAD_DIM), 1.0, 5.0, ((0, 8), (1, 2))),
        "home_value": centred(part_splits[2], (REQS, KV_HEADS * HEAD_DIM), 1.0, 5.0, ((0, 8), (1, 2))),
        "cache_keys": draw_cache_keys(jax.random.fold_in(jax.random.fold_in(splits[12], part), 71), part),
        "cache_values": centred(part_splits[4], (N_POOL * CAP, KV_HEADS * HEAD_DIM), 1.0, 5.0, ((0, 8), (1, 2))),
        "cache_start": draw_cache_start(jax.random.fold_in(jax.random.fold_in(splits[12], part), 71), part),
        "cache_len": draw_cache_len(jax.random.fold_in(jax.random.fold_in(splits[12], part), 71), part),
        "prompt_query": draw_prompt_query(jax.random.fold_in(jax.random.fold_in(splits[12], part), 71), part),
        "prompt_key": draw_prompt_key(jax.random.fold_in(jax.random.fold_in(splits[12], part), 71), part),
        "prompt_value": centred(part_splits[9], (N_POOL * PRE_DEV, KV_HEADS * HEAD_DIM), 1.0, 5.0, ((0, 8), (1, 2))),
        "doc_ids": jax.vmap(lambda own: jnp.searchsorted(jnp.cumsum(ragged_sizes(own, DOCS, PRE_DEV, PRE_DEV // 2, 1)), jnp.arange(PRE_DEV), side="right"))(jax.random.split(part_splits[10], N_POOL)).reshape((N_POOL, PRE_DEV)).astype(jnp.int32),
        "out_weight": centred(splits[11], (D, D), D ** -0.5, 0.0625, ((0, 2), (1, 8))),
    }


def prompt_block(block):
    query, keys, values, doc_row = block
    row_count = query.shape[0]
    group_size = HEADS // KV_HEADS
    query_heads = query.astype(jnp.float32).reshape(row_count, KV_HEADS, group_size, HEAD_DIM)
    key_heads = keys.astype(jnp.float32).reshape(row_count, KV_HEADS, HEAD_DIM)
    value_heads = values.astype(jnp.float32).reshape(row_count, KV_HEADS, HEAD_DIM)
    scores = jnp.einsum('ikgd,jkd->kgij', query_heads, key_heads) * (HEAD_DIM ** -0.5)
    positions = jnp.arange(row_count, dtype=jnp.int32)
    allowed = (positions[:, None] >= positions[None, :]) & (doc_row[:, None] == doc_row[None, :])
    scores = jnp.where(allowed[None, None], scores, -jnp.inf)
    highest = jnp.max(scores, axis=-1, keepdims=True)
    weights = jnp.exp(scores - highest)
    probabilities = (weights / jnp.sum(weights, axis=-1, keepdims=True)).astype(jnp.bfloat16)
    result = jnp.einsum('kgij,jkd->ikgd', probabilities.astype(jnp.float32), value_heads)
    return result.astype(jnp.bfloat16).reshape(row_count, D)


def reference(home_query, home_key, home_value, cache_keys, cache_values, cache_start, cache_len, prompt_query, prompt_key, prompt_value, doc_ids, out_weight):
    prompt_out = lax.map(prompt_block, (prompt_query.reshape(N_POOL, PRE_DEV, D),
                                        prompt_key.reshape(N_POOL, PRE_DEV, KV_HEADS * HEAD_DIM),
                                        prompt_value.reshape(N_POOL, PRE_DEV, KV_HEADS * HEAD_DIM),
                                        doc_ids)).reshape(N_POOL * PRE_DEV, D)
    group_size = HEADS // KV_HEADS
    score_scale = HEAD_DIM ** -0.5

    def one_request(request):
        query, key_new, value_new, first_row, length = request
        first_row = first_row.astype(jnp.int32)
        window = jnp.minimum(first_row, N_POOL * CAP - CACHE_MAX).astype(jnp.int32)
        keys = lax.dynamic_slice_in_dim(cache_keys, window, CACHE_MAX, 0).astype(jnp.float32).reshape(CACHE_MAX, KV_HEADS, HEAD_DIM)
        values = lax.dynamic_slice_in_dim(cache_values, window, CACHE_MAX, 0).astype(jnp.float32).reshape(CACHE_MAX, KV_HEADS, HEAD_DIM)
        positions = window + jnp.arange(CACHE_MAX, dtype=jnp.int32)
        in_segment = (positions >= first_row) & (positions < first_row + length)
        query_heads = query.astype(jnp.float32).reshape(KV_HEADS, group_size, HEAD_DIM)
        scores = jnp.einsum('kgd,ckd->kgc', query_heads, keys) * score_scale
        scores = jnp.where(in_segment[None, None, :], scores, -jnp.inf)
        own_score = jnp.einsum('kgd,kd->kg', query_heads, key_new.astype(jnp.float32).reshape(KV_HEADS, HEAD_DIM)) * score_scale
        highest = jnp.maximum(jnp.max(scores, axis=-1), own_score)
        cache_weights = jnp.exp(scores - highest[..., None])
        own_weight = jnp.exp(own_score - highest)
        denominator = jnp.sum(cache_weights, axis=-1) + own_weight
        cache_probs = (cache_weights / denominator[..., None]).astype(jnp.bfloat16)
        own_prob = (own_weight / denominator).astype(jnp.bfloat16)
        result = jnp.einsum('kgc,ckd->kgd', cache_probs.astype(jnp.float32), values)
        result = result + own_prob.astype(jnp.float32)[..., None] * value_new.astype(jnp.float32).reshape(KV_HEADS, 1, HEAD_DIM)
        return result.astype(jnp.bfloat16).reshape(D)

    attended = lax.map(one_request, (home_query, home_key, home_value, cache_start, cache_len))
    decode_out = jnp.dot(attended, out_weight, preferred_element_type=jnp.float32).astype(jnp.bfloat16)
    return prompt_out, decode_out
```

```python
import functools
import math

import jax
import jax.numpy as jnp
from jax import lax
from jax.experimental import pallas as pl
from jax.experimental.pallas import tpu as pltpu
from jax.sharding import PartitionSpec as P

HEAD_DIM = 128
LANES = 128
ROW_BLOCK = 32
MASKED = -1e30
SCALE = HEAD_DIM ** (-0.5)
F32 = jnp.float32
BF16 = jnp.bfloat16
MESH = pl.DeviceIdType.MESH
NT = (((1,), (1,)), ((), ()))


def windows(rows):
    width = -(-(rows // 2 + ROW_BLOCK) // LANES) * LANES
    out = []
    for first in range(0, rows, ROW_BLOCK):
        end = first + ROW_BLOCK
        low = max(0, end - width)
        high = min(rows, max(end, low + -(-(end - low) // LANES) * LANES))
        out.append((first, low, high))
    return width, out


def fill_bias(doc_ref, bias_ref):
    rows = doc_ref.shape[1]
    for first, low, high in windows(rows)[1]:
        span = high - low
        row_at = first + lax.broadcasted_iota(jnp.int32, (ROW_BLOCK, span), 0)
        col_at = low + lax.broadcasted_iota(jnp.int32, (ROW_BLOCK, span), 1)
        doc = jnp.broadcast_to(doc_ref[:, low:high], (ROW_BLOCK, span)).astype(F32)
        own = jnp.sum(jnp.where(row_at == col_at, doc, 0.0), axis=1, keepdims=True)
        allowed = (col_at <= row_at) & (doc == own)
        bias_ref[first : first + ROW_BLOCK, :span] = jnp.where(allowed, 0.0, MASKED)


def prompt_group(query, key, value, bias_ref, wide_ref, out, group_size):
    rows = key.shape[0]
    wide_ref[:, :HEAD_DIM] = value[...]
    factor = SCALE * math.log2(math.e)
    for first, low, high in windows(rows)[1]:
        span = high - low
        block = slice(first, first + ROW_BLOCK)
        stacked = jnp.concatenate(
            [query[block, h * HEAD_DIM : (h + 1) * HEAD_DIM] for h in range(group_size)], axis=0
        )
        scores = lax.dot_general(stacked, key[low:high, :], NT, preferred_element_type=F32)
        scores = scores.reshape(group_size, ROW_BLOCK, span) + bias_ref[block, :span][None]
        highest = jnp.max(scores, axis=-1, keepdims=True)
        weights = jnp.exp2((scores - highest) * factor).astype(BF16)
        weights = weights.reshape(group_size * ROW_BLOCK, span)
        result = jnp.dot(weights, wide_ref[low:high, :], preferred_element_type=F32)
        result = (result[:, :HEAD_DIM] / result[:, HEAD_DIM:]).astype(BF16)
        for h in range(group_size):
            out[block, h * HEAD_DIM : (h + 1) * HEAD_DIM] = result[
                h * ROW_BLOCK : (h + 1) * ROW_BLOCK
            ]


def prompt_kernel(group_size, doc_ref, q_ref, k_ref, v_ref, o_ref, bias_ref, wide_ref):
    @pl.when(pl.program_id(0) == 0)
    def _():
        fill_bias(doc_ref, bias_ref)
        wide_ref[:, HEAD_DIM:] = jnp.ones((wide_ref.shape[0], HEAD_DIM), BF16)

    prompt_group(q_ref, k_ref, v_ref, bias_ref, wide_ref, o_ref, group_size)


def prompt_attention(prompt_query, prompt_key, prompt_value, doc_ids):
    rows = prompt_query.shape[0]
    kv_local = prompt_key.shape[1] // HEAD_DIM
    width = prompt_query.shape[1] // kv_local
    return pl.pallas_call(
        functools.partial(prompt_kernel, width // HEAD_DIM),
        grid=(kv_local,),
        out_shape=jax.ShapeDtypeStruct(prompt_query.shape, BF16),
        in_specs=[
            pl.BlockSpec((1, rows), lambda g: (0, 0)),
            pl.BlockSpec((rows, width), lambda g: (0, g)),
            pl.BlockSpec((rows, HEAD_DIM), lambda g: (0, g)),
            pl.BlockSpec((rows, HEAD_DIM), lambda g: (0, g)),
        ],
        out_specs=pl.BlockSpec((rows, width), lambda g: (0, g)),
        scratch_shapes=[
            pltpu.VMEM((rows, windows(rows)[0]), F32),
            pltpu.VMEM((rows, 2 * HEAD_DIM), BF16),
        ],
        compiler_params=pltpu.CompilerParams(vmem_limit_bytes=40 * 1024 * 1024),
    )(doc_ids, prompt_query, prompt_key, prompt_value)


def routing(start_row, len_row, me, cap_rows, n, slots):
    total = start_row.shape[1]
    owner = jnp.zeros_like(start_row)
    for p in range(1, n):
        owner = owner + (start_row >= p * cap_rows).astype(jnp.int32)
    owner = jnp.broadcast_to(owner, (total, total)).astype(F32)
    at_row = lax.broadcasted_iota(jnp.int32, (total, total), 0)
    at_col = lax.broadcasted_iota(jnp.int32, (total, total), 1)
    same = at_row == at_col
    owner_col = jnp.sum(jnp.where(same, owner, 0.0), axis=1, keepdims=True)
    together = owner == owner_col
    rank = jnp.sum(jnp.where(together & (at_row < at_col), 1.0, 0.0), axis=0, keepdims=True)
    rank_col = jnp.sum(jnp.where(together & (at_col < at_row), 1.0, 0.0), axis=1, keepdims=True)
    slot_at = lax.broadcasted_iota(jnp.int32, (slots, total), 0).astype(F32)
    mine = (owner[:1] == me.astype(F32)) & (rank == slot_at)
    first = jnp.sum(jnp.where(mine, start_row - me * cap_rows, 0), axis=1, keepdims=True)
    length = jnp.sum(jnp.where(mine, len_row, 0), axis=1, keepdims=True)
    place = lax.broadcasted_iota(jnp.int32, (total, n * slots), 1).astype(F32)
    unpack = jnp.where(owner_col * slots + rank_col == place, 1.0, 0.0).astype(BF16)
    return jnp.where(mine, 1.0, 0.0).astype(BF16), first, length, unpack


def slot_rows(select, gathered, flat):
    n, rows, width = gathered.shape
    for s in range(n):
        flat[s * rows : (s + 1) * rows, :width] = gathered[s].astype(F32)
    return jnp.dot(select, flat[:, :width].astype(BF16), preferred_element_type=F32)


def decode_kernel(
    n, tps, start_ref, len_ref, hq, hk, hv, ck_hbm, cv_hbm, w_hbm, out_ref,
    all_q, all_k, all_v, flat, ck, cv, w, pooled, part, part_in,
    load_sem, w_sem, send_sem, recv_sem, out_send, out_recv, tp_send, tp_recv,
):
    me, tpi = lax.axis_index("pool"), lax.axis_index("tp")
    slots = pooled.shape[1]
    cap_rows = ck.shape[0]
    kv_local = ck.shape[1] // HEAD_DIM
    group_size = hq.shape[1] // ck.shape[1]
    pieces = w_sem.shape[0]
    depth = w.shape[0] // pieces

    barrier = pltpu.get_barrier_semaphore()
    for d in range(1, n):
        pl.semaphore_signal(
            barrier, inc=1, device_id={"pool": lax.rem(me + d, n)}, device_id_type=MESH
        )
    for d in range(1, tps):
        pl.semaphore_signal(
            barrier, inc=1, device_id={"tp": lax.rem(tpi + d, tps)}, device_id_type=MESH
        )
    loads = [
        pltpu.make_async_copy(src, dst, load_sem.at[i])
        for i, (src, dst) in enumerate(
            [(hq, all_q.at[me]), (hk, all_k.at[me]), (hv, all_v.at[me]), (ck_hbm, ck), (cv_hbm, cv)]
        )
    ]
    for load in loads:
        load.start()
    w_loads = [
        pltpu.make_async_copy(
            w_hbm.at[i * depth : (i + 1) * depth], w.at[i * depth : (i + 1) * depth], w_sem.at[i]
        )
        for i in range(pieces)
    ]
    for load in w_loads:
        load.start()
    pl.semaphore_wait(barrier, n - 1 + tps - 1)
    sends = []
    for d in range(1, n):
        for i, (src, dst) in enumerate([(hq, all_q), (hk, all_k), (hv, all_v)]):
            sends.append(
                pltpu.make_async_remote_copy(
                    src_ref=src, dst_ref=dst.at[me],
                    send_sem=send_sem.at[i, d], recv_sem=recv_sem.at[i, d],
                    device_id={"pool": lax.rem(me + d, n)}, device_id_type=MESH,
                )
            )
            sends[-1].start()

    select, first, length, unpack = routing(start_ref[...], len_ref[...], me, cap_rows, n, slots)
    at = lax.broadcasted_iota(jnp.int32, (slots, cap_rows), 1)
    bias = jnp.where((at >= first) & (at < first + length), 0.0, MASKED)
    bias = jnp.concatenate([bias] * group_size, axis=0)

    for load in loads:
        load.wait()
    for send in sends:
        send.wait()
    slot_key = slot_rows(select, all_k, flat)
    slot_value = slot_rows(select, all_v, flat)
    slot_query = slot_rows(select, all_q, flat)
    for g in range(kv_local):
        lanes = slice(g * HEAD_DIM, (g + 1) * HEAD_DIM)
        base = g * group_size * HEAD_DIM
        query = jnp.concatenate(
            [
                slot_query[:, base + h * HEAD_DIM : base + (h + 1) * HEAD_DIM]
                for h in range(group_size)
            ],
            axis=0,
        )
        scores = (
            lax.dot_general(query.astype(BF16), ck[:, lanes], NT, preferred_element_type=F32)
            * SCALE
            + bias
        )
        own_key = jnp.concatenate([slot_key[:, lanes]] * group_size, axis=0)
        own_value = jnp.concatenate([slot_value[:, lanes]] * group_size, axis=0)
        own = jnp.sum(query * own_key, axis=1, keepdims=True) * SCALE
        highest = jnp.maximum(jnp.max(scores, axis=1, keepdims=True), own)
        weights = jnp.exp(scores - highest)
        own_weight = jnp.exp(own - highest)
        total = jnp.sum(weights, axis=1, keepdims=True) + own_weight
        probs = (weights / total).astype(BF16)
        own_prob = (own_weight / total).astype(BF16).astype(F32)
        result = jnp.dot(probs, cv[:, lanes], preferred_element_type=F32) + own_prob * own_value
        for h in range(group_size):
            pooled[me, :, base + h * HEAD_DIM : base + (h + 1) * HEAD_DIM] = result[
                h * slots : (h + 1) * slots
            ].astype(BF16)

    sends = []
    for d in range(1, n):
        sends.append(
            pltpu.make_async_remote_copy(
                src_ref=pooled.at[me], dst_ref=pooled.at[me],
                send_sem=out_send.at[d], recv_sem=out_recv.at[d],
                device_id={"pool": lax.rem(me + d, n)}, device_id_type=MESH,
            )
        )
        sends[-1].start()
    for load in w_loads:
        load.wait()
    for send in sends:
        send.wait()
    sums = None
    for i in range(pieces):
        span = slice(i * depth, (i + 1) * depth)
        joined = jnp.concatenate([pooled[s, :, span].astype(F32) for s in range(n)], axis=0)
        attended = jnp.dot(unpack, joined.astype(BF16), preferred_element_type=F32).astype(BF16)
        term = jnp.dot(attended, w[span, :], preferred_element_type=F32)
        sums = term if sums is None else sums + term
    rows = part.shape[1]
    for t in range(tps):
        part[t] = sums[t * rows : (t + 1) * rows]
    sends = []
    for d in range(1, tps):
        peer = lax.rem(tpi + d, tps)
        sends.append(
            pltpu.make_async_remote_copy(
                src_ref=part.at[peer], dst_ref=part_in.at[d],
                send_sem=tp_send.at[d], recv_sem=tp_recv.at[d],
                device_id={"tp": peer}, device_id_type=MESH,
            )
        )
        sends[-1].start()
    for send in sends:
        send.wait()
    total = part[tpi]
    for d in range(1, tps):
        total = total + part_in[d]
    out_ref[...] = total.astype(BF16)


def decode(
    n, tps, home_query, home_key, home_value, cache_keys, cache_values, start, length, out_weight
):
    requests = start.shape[0]
    home_rows, width = home_query.shape
    kv_width = home_key.shape[1]
    slots = 2 * home_rows
    out_rows, out_cols = requests // tps, out_weight.shape[1]
    pieces = 4
    vmem, hbm = pl.BlockSpec(memory_space=pltpu.VMEM), pl.BlockSpec(memory_space=pl.ANY)
    dma = pltpu.SemaphoreType.DMA
    return pl.pallas_call(
        functools.partial(decode_kernel, n, tps),
        out_shape=jax.ShapeDtypeStruct((out_rows, out_cols), BF16),
        in_specs=[vmem, vmem] + [hbm] * 6,
        out_specs=vmem,
        scratch_shapes=[
            pltpu.VMEM((n, home_rows, width), BF16),
            pltpu.VMEM((n, home_rows, kv_width), BF16),
            pltpu.VMEM((n, home_rows, kv_width), BF16),
            pltpu.VMEM((requests, width), F32),
            pltpu.VMEM(cache_keys.shape, BF16),
            pltpu.VMEM(cache_values.shape, BF16),
            pltpu.VMEM(out_weight.shape, BF16),
            pltpu.VMEM((n, slots, width), BF16),
            pltpu.VMEM((tps, out_rows, out_cols), F32),
            pltpu.VMEM((tps, out_rows, out_cols), F32),
            dma((5,)), dma((pieces,)), dma((3, n)), dma((3, n)),
            dma((n,)), dma((n,)), dma((tps,)), dma((tps,)),
        ],
        compiler_params=pltpu.CompilerParams(
            collective_id=0, has_side_effects=True, vmem_limit_bytes=40 * 1024 * 1024
        ),
    )(
        start.reshape(1, requests), length.reshape(1, requests),
        home_query, home_key, home_value, cache_keys, cache_values, out_weight,
    )


def solution(mesh):
    n, tps = mesh.shape["pool"], mesh.shape["tp"]

    def local(
        home_query, home_key, home_value, cache_keys, cache_values, cache_start, cache_len,
        prompt_query, prompt_key, prompt_value, doc_ids, out_weight,
    ):
        decode_out = decode(
            n, tps, home_query, home_key, home_value, cache_keys, cache_values,
            cache_start, cache_len, out_weight,
        )
        prompt_out = prompt_attention(prompt_query, prompt_key, prompt_value, doc_ids)
        return prompt_out, decode_out

    return jax.shard_map(
        local,
        mesh=mesh,
        in_specs=(
            P(("grp", "pool"), "tp"),
            P(("grp", "pool"), "tp"),
            P(("grp", "pool"), "tp"),
            P(("grp", "pool"), "tp"),
            P(("grp", "pool"), "tp"),
            P("grp"),
            P("grp"),
            P(("grp", "pool"), "tp"),
            P(("grp", "pool"), "tp"),
            P(("grp", "pool"), "tp"),
            P(("grp", "pool"), None),
            P("tp", "pool"),
        ),
        out_specs=(P(("grp", "pool"), "tp"), P(("grp", "tp"), "pool")),
        check_vma=False,
    )
```

```python
import functools
import math

import jax
import jax.numpy as jnp
from jax import lax
from jax.experimental import pallas as pl
from jax.experimental.pallas import tpu as pltpu
from jax.sharding import PartitionSpec as P

HEAD_DIM = 128
LANES = 128
ROW_BLOCK = 32
MASKED = -1e30
SHARES = (0.0, 0.3, 0.45, 0.8, 0.92, 1.0)
SCALE = HEAD_DIM ** (-0.5)
F32 = jnp.float32
BF16 = jnp.bfloat16
MESH = pl.DeviceIdType.MESH
NT = (((1,), (1,)), ((), ()))


def windows(rows):
    width = -(-(rows // 2 + ROW_BLOCK) // LANES) * LANES
    out = []
    for first in range(0, rows, ROW_BLOCK):
        end = first + ROW_BLOCK
        low = max(0, end - width)
        high = min(rows, max(end, low + -(-(end - low) // LANES) * LANES))
        out.append((first, low, high))
    return width, out


def fill_bias(doc_ref, bias_ref):
    rows = doc_ref.shape[1]
    for first, low, high in windows(rows)[1]:
        span = high - low
        row_at = first + lax.broadcasted_iota(jnp.int32, (ROW_BLOCK, span), 0)
        col_at = low + lax.broadcasted_iota(jnp.int32, (ROW_BLOCK, span), 1)
        doc = jnp.broadcast_to(doc_ref[:, low:high], (ROW_BLOCK, span)).astype(F32)
        own = jnp.sum(jnp.where(row_at == col_at, doc, 0.0), axis=1, keepdims=True)
        allowed = (col_at <= row_at) & (doc == own)
        bias_ref[first : first + ROW_BLOCK, :span] = jnp.where(allowed, 0.0, MASKED)


def prompt_blocks(query, key, value, bias_ref, wide_ref, out, group_size, head_group, blocks):
    rows = key.shape[0]
    lanes = slice(head_group * HEAD_DIM, (head_group + 1) * HEAD_DIM)
    base = head_group * group_size * HEAD_DIM
    factor = SCALE * math.log2(math.e)
    for first, low, high in blocks:
        if first == 0:
            wide_ref[:, :HEAD_DIM] = value[:, lanes]
        span = high - low
        block = slice(first, first + ROW_BLOCK)
        heads = [slice(base + h * HEAD_DIM, base + (h + 1) * HEAD_DIM) for h in range(group_size)]
        stacked = jnp.concatenate([query[block, head] for head in heads], axis=0)
        scores = lax.dot_general(stacked, key[low:high, lanes], NT, preferred_element_type=F32)
        scores = scores.reshape(group_size, ROW_BLOCK, span) + bias_ref[block, :span][None]
        highest = jnp.max(scores, axis=-1, keepdims=True)
        weights = jnp.exp2((scores - highest) * factor).astype(BF16)
        weights = weights.reshape(group_size * ROW_BLOCK, span)
        result = jnp.dot(weights, wide_ref[low:high, :], preferred_element_type=F32)
        result = (result[:, :HEAD_DIM] / result[:, HEAD_DIM:]).astype(BF16)
        for h, head in enumerate(heads):
            out[block, head] = result[h * ROW_BLOCK : (h + 1) * ROW_BLOCK]


def routing(start_row, len_row, me, cap_rows, n, slots):
    total = start_row.shape[1]
    owner = jnp.zeros_like(start_row)
    for p in range(1, n):
        owner = owner + (start_row >= p * cap_rows).astype(jnp.int32)
    owner = jnp.broadcast_to(owner, (total, total)).astype(F32)
    at_row = lax.broadcasted_iota(jnp.int32, (total, total), 0)
    at_col = lax.broadcasted_iota(jnp.int32, (total, total), 1)
    same = at_row == at_col
    owner_col = jnp.sum(jnp.where(same, owner, 0.0), axis=1, keepdims=True)
    together = owner == owner_col
    rank = jnp.sum(jnp.where(together & (at_row < at_col), 1.0, 0.0), axis=0, keepdims=True)
    rank_col = jnp.sum(jnp.where(together & (at_col < at_row), 1.0, 0.0), axis=1, keepdims=True)
    slot_at = lax.broadcasted_iota(jnp.int32, (slots, total), 0).astype(F32)
    mine = (owner[:1] == me.astype(F32)) & (rank == slot_at)
    first = jnp.sum(jnp.where(mine, start_row - me * cap_rows, 0), axis=1, keepdims=True)
    length = jnp.sum(jnp.where(mine, len_row, 0), axis=1, keepdims=True)
    place = lax.broadcasted_iota(jnp.int32, (total, n * slots), 1).astype(F32)
    unpack = jnp.where(owner_col * slots + rank_col == place, 1.0, 0.0).astype(BF16)
    return jnp.where(mine, 1.0, 0.0).astype(BF16), first, length, unpack


def slot_rows(select, gathered, flat):
    n, rows, width = gathered.shape
    for s in range(n):
        flat[s * rows : (s + 1) * rows, :width] = gathered[s].astype(F32)
    return jnp.dot(select, flat[:, :width].astype(BF16), preferred_element_type=F32)


def spread(buffers, mine, direct, relay, me, n):
    partner = me + 1 - 2 * lax.rem(me, 2)
    firsts, relays = [], []
    for d in range(n // 2):
        peer = partner if d == 0 else lax.rem(me + 2 * d, n)
        origin = lax.rem(me - 2 * d + n, n)
        for i, (buffer, block) in enumerate(zip(buffers, mine)):
            firsts.append(
                pltpu.make_async_remote_copy(
                    src_ref=block, dst_ref=buffer.at[me],
                    send_sem=direct.at[0, i, d], recv_sem=direct.at[1, i, d],
                    device_id={"pool": peer}, device_id_type=MESH,
                )
            )
            if d > 0:
                relays.append(
                    pltpu.make_async_remote_copy(
                        src_ref=buffer.at[origin], dst_ref=buffer.at[origin],
                        send_sem=relay.at[0, i, d], recv_sem=relay.at[1, i, d],
                        device_id={"pool": partner}, device_id_type=MESH,
                    )
                )
    return firsts, relays


def start_relays(firsts, relays):
    skip = len(firsts) - len(relays)
    for first, relay in zip(firsts[skip:], relays):
        first.wait_recv()
        relay.start()


def step_kernel(
    n, tps, shares, start_ref, len_ref, doc_ref, hq, hk, hv, ck_hbm, cv_hbm, w_hbm,
    pq_hbm, pk_hbm, pv_hbm, out_ref, prompt_ref,
    all_q, all_k, all_v, flat, ck, cv, w, pooled, part, part_in,
    pq, pk, pv, prompt_out, bias_ref, wide_ref,
    load_sem, w_sem, pq_sem, store_sem, direct_sem, relay_sem, out_direct, out_relay,
    tp_send, tp_recv,
):
    me, tpi = lax.axis_index("pool"), lax.axis_index("tp")
    slots = pooled.shape[1]
    cap_rows = ck.shape[0]
    kv_local = ck.shape[1] // HEAD_DIM
    group_size = hq.shape[1] // ck.shape[1]
    group_width = group_size * HEAD_DIM
    pieces = w_sem.shape[0]
    depth = w.shape[0] // pieces

    barrier = pltpu.get_barrier_semaphore()
    for d in range(n // 2):
        peer = me + 1 - 2 * lax.rem(me, 2) if d == 0 else lax.rem(me + 2 * d, n)
        pl.semaphore_signal(barrier, inc=1, device_id={"pool": peer}, device_id_type=MESH)
    for d in range(1, tps):
        pl.semaphore_signal(
            barrier, inc=1, device_id={"tp": lax.rem(tpi + d, tps)}, device_id_type=MESH
        )
    loads = [
        pltpu.make_async_copy(src, dst, load_sem.at[i])
        for i, (src, dst) in enumerate(
            [
                (pk_hbm, pk), (pv_hbm, pv), (hq, all_q.at[me]), (hk, all_k.at[me]),
                (hv, all_v.at[me]), (ck_hbm, ck), (cv_hbm, cv),
            ]
        )
    ]
    groups = [slice(g * group_width, (g + 1) * group_width) for g in range(kv_local)]
    pq_loads = [
        pltpu.make_async_copy(pq_hbm.at[:, span], pq.at[:, span], pq_sem.at[g])
        for g, span in enumerate(groups)
    ]
    stores = [
        pltpu.make_async_copy(prompt_out.at[:, span], prompt_ref.at[:, span], store_sem.at[g])
        for g, span in enumerate(groups)
    ]
    w_loads = [
        pltpu.make_async_copy(
            w_hbm.at[i * depth : (i + 1) * depth], w.at[i * depth : (i + 1) * depth], w_sem.at[i]
        )
        for i in range(pieces)
    ]
    for load in loads[:2] + pq_loads[:1] + loads[2:] + pq_loads[1:] + w_loads:
        load.start()

    blocks = windows(pk.shape[0])[1]
    work = [(g, block) for g in range(kv_local) for block in blocks]

    def prompt_share(share):
        low, high = (round(len(work) * shares[share + k]) for k in range(2))
        for g, block in work[low:high]:
            if block is blocks[0]:
                pq_loads[g].wait()
            prompt_blocks(
                pq, pk, pv, bias_ref, wide_ref, prompt_out, group_size, g, [block]
            )
            if block is blocks[-1]:
                stores[g].start()

    pl.semaphore_wait(barrier, n // 2 + tps - 1)
    firsts, relays = spread(
        (all_q, all_k, all_v), (hq, hk, hv), direct_sem, relay_sem, me, n
    )
    for copy in firsts:
        copy.start()
    fill_bias(doc_ref, bias_ref)
    wide_ref[:, HEAD_DIM:] = jnp.ones((wide_ref.shape[0], HEAD_DIM), BF16)
    for load in loads:
        load.wait()
    select, first, length, unpack = routing(start_ref[...], len_ref[...], me, cap_rows, n, slots)
    at = lax.broadcasted_iota(jnp.int32, (slots, cap_rows), 1)
    bias = jnp.where((at >= first) & (at < first + length), 0.0, MASKED)
    bias = jnp.concatenate([bias] * group_size, axis=0)

    prompt_share(0)
    start_relays(firsts, relays)
    prompt_share(1)
    for copy in firsts[: len(firsts) - len(relays)] + relays:
        copy.wait_recv()
    slot_key = slot_rows(select, all_k, flat)
    slot_value = slot_rows(select, all_v, flat)
    slot_query = slot_rows(select, all_q, flat)
    for g in range(kv_local):
        lanes = slice(g * HEAD_DIM, (g + 1) * HEAD_DIM)
        base = g * group_size * HEAD_DIM
        query = jnp.concatenate(
            [
                slot_query[:, base + h * HEAD_DIM : base + (h + 1) * HEAD_DIM]
                for h in range(group_size)
            ],
            axis=0,
        )
        scores = (
            lax.dot_general(query.astype(BF16), ck[:, lanes], NT, preferred_element_type=F32)
            * SCALE
            + bias
        )
        own_key = jnp.concatenate([slot_key[:, lanes]] * group_size, axis=0)
        own_value = jnp.concatenate([slot_value[:, lanes]] * group_size, axis=0)
        own = jnp.sum(query * own_key, axis=1, keepdims=True) * SCALE
        highest = jnp.maximum(jnp.max(scores, axis=1, keepdims=True), own)
        weights = jnp.exp(scores - highest)
        own_weight = jnp.exp(own - highest)
        total = jnp.sum(weights, axis=1, keepdims=True) + own_weight
        probs = (weights / total).astype(BF16)
        own_prob = (own_weight / total).astype(BF16).astype(F32)
        result = jnp.dot(probs, cv[:, lanes], preferred_element_type=F32) + own_prob * own_value
        for h in range(group_size):
            pooled[me, :, base + h * HEAD_DIM : base + (h + 1) * HEAD_DIM] = result[
                h * slots : (h + 1) * slots
            ].astype(BF16)

    out_firsts, out_relays = spread((pooled,), (pooled.at[me],), out_direct, out_relay, me, n)
    for copy in out_firsts:
        copy.start()
    prompt_share(2)
    start_relays(out_firsts, out_relays)
    prompt_share(3)
    for load in w_loads:
        load.wait()
    for copy in out_firsts[: len(out_firsts) - len(out_relays)] + out_relays:
        copy.wait_recv()
    sums = None
    for i in range(pieces):
        span = slice(i * depth, (i + 1) * depth)
        joined = jnp.concatenate([pooled[s, :, span].astype(F32) for s in range(n)], axis=0)
        attended = jnp.dot(unpack, joined.astype(BF16), preferred_element_type=F32).astype(BF16)
        term = jnp.dot(attended, w[span, :], preferred_element_type=F32)
        sums = term if sums is None else sums + term
    rows = part.shape[1]
    for t in range(tps):
        part[t] = sums[t * rows : (t + 1) * rows]
    sends = []
    for d in range(1, tps):
        peer = lax.rem(tpi + d, tps)
        sends.append(
            pltpu.make_async_remote_copy(
                src_ref=part.at[peer], dst_ref=part_in.at[d],
                send_sem=tp_send.at[d], recv_sem=tp_recv.at[d],
                device_id={"tp": peer}, device_id_type=MESH,
            )
        )
        sends[-1].start()
    prompt_share(4)
    for copy in firsts + relays + out_firsts + out_relays:
        copy.wait_send()
    for send in sends:
        send.wait()
    total = part[tpi]
    for d in range(1, tps):
        total = total + part_in[d]
    out_ref[...] = total.astype(BF16)
    for store in stores:
        store.wait()


def step(
    n, tps, home_query, home_key, home_value, cache_keys, cache_values, start, length,
    prompt_query, prompt_key, prompt_value, doc_ids, out_weight,
):
    requests = start.shape[0]
    home_rows, width = home_query.shape
    kv_width = home_key.shape[1]
    kv_local = kv_width // HEAD_DIM
    rows = prompt_query.shape[0]
    slots = 2 * home_rows
    out_rows, out_cols = requests // tps, out_weight.shape[1]
    pieces = 4
    vmem, hbm = pl.BlockSpec(memory_space=pltpu.VMEM), pl.BlockSpec(memory_space=pltpu.HBM)
    dma = pltpu.SemaphoreType.DMA
    half = n // 2
    decode_out, prompt_out = pl.pallas_call(
        functools.partial(step_kernel, n, tps, SHARES),
        out_shape=[
            jax.ShapeDtypeStruct((out_rows, out_cols), BF16),
            jax.ShapeDtypeStruct(prompt_query.shape, BF16),
        ],
        in_specs=[vmem] * 3 + [hbm] * 9,
        out_specs=[vmem, hbm],
        scratch_shapes=[
            pltpu.VMEM((n, home_rows, width), BF16),
            pltpu.VMEM((n, home_rows, kv_width), BF16),
            pltpu.VMEM((n, home_rows, kv_width), BF16),
            pltpu.VMEM((requests, width), F32),
            pltpu.VMEM(cache_keys.shape, BF16),
            pltpu.VMEM(cache_values.shape, BF16),
            pltpu.VMEM(out_weight.shape, BF16),
            pltpu.VMEM((n, slots, width), BF16),
            pltpu.VMEM((tps, out_rows, out_cols), F32),
            pltpu.VMEM((tps, out_rows, out_cols), F32),
            pltpu.VMEM(prompt_query.shape, BF16),
            pltpu.VMEM(prompt_key.shape, BF16),
            pltpu.VMEM(prompt_value.shape, BF16),
            pltpu.VMEM(prompt_query.shape, BF16),
            pltpu.VMEM((rows, windows(rows)[0]), F32),
            pltpu.VMEM((rows, 2 * HEAD_DIM), BF16),
            dma((7,)), dma((pieces,)), dma((kv_local,)), dma((kv_local,)),
            dma((2, 3, half)), dma((2, 3, half)), dma((2, 1, half)), dma((2, 1, half)),
            dma((tps,)), dma((tps,)),
        ],
        compiler_params=pltpu.CompilerParams(
            collective_id=0, has_side_effects=True, vmem_limit_bytes=60 * 1024 * 1024
        ),
    )(
        start.reshape(1, requests), length.reshape(1, requests), doc_ids,
        home_query, home_key, home_value, cache_keys, cache_values, out_weight,
        prompt_query, prompt_key, prompt_value,
    )
    return prompt_out, decode_out


def solution(mesh):
    n, tps = mesh.shape["pool"], mesh.shape["tp"]

    def local(
        home_query, home_key, home_value, cache_keys, cache_values, cache_start, cache_len,
        prompt_query, prompt_key, prompt_value, doc_ids, out_weight,
    ):
        return step(
            n, tps, home_query, home_key, home_value, cache_keys, cache_values,
            cache_start, cache_len, prompt_query, prompt_key, prompt_value, doc_ids, out_weight,
        )

    return jax.shard_map(
        local,
        mesh=mesh,
        in_specs=(
            P(("grp", "pool"), "tp"),
            P(("grp", "pool"), "tp"),
            P(("grp", "pool"), "tp"),
            P(("grp", "pool"), "tp"),
            P(("grp", "pool"), "tp"),
            P("grp"),
            P("grp"),
            P(("grp", "pool"), "tp"),
            P(("grp", "pool"), "tp"),
            P(("grp", "pool"), "tp"),
            P(("grp", "pool"), None),
            P("tp", "pool"),
        ),
        out_specs=(P(("grp", "pool"), "tp"), P(("grp", "tp"), "pool")),
        check_vma=False,
    )
```
